32 devices in a mesh: sx: 4 (over z), sy: 8 (over y, x, core).
Axes of the slice: x: 2, y: 2, z: 4, core: 2. Of those that a mesh axis runs over, the one named last changes fastest.
Arguments:
- residual: bfloat16 [4, 8, 2048, 128], P('sx', 'sy'), may hold values from -6 to 6
- weights: float32 [4, 8, 2048], P('sx', 'sy'), may hold values from 0.1 to 1.9
- blocks: bfloat16 [4, 8, 16, 4, 128, 128], P('sx', 'sy'), may hold values from -0.25 to 0.25
- pattern: int32 [4, 8, 16, 4], P('sx', 'sy'), may hold values from 0 to 15
- primal_basis: bfloat16 [4, 8, 2048, 64], P('sx', 'sy'), may hold values from -0.25 to 0.25
- coarse_inverse: float32 [4, 512, 512], P('sx', 'sy'), may hold values from -0.25 to 0.25
- coarse_rows: int32 [4, 512], P('sx'), may hold values from 0 to 511, each once within a row
- shared_lists: int32 [4, 8, 4, 512], P('sx', 'sy'), may hold values from 0 to 511, each once within a row
Outputs:
- preconditioned: bfloat16 [4, 8, 2048, 128], P('sx', 'sy')
The draws below stay inside these ranges and needn't reach their ends.
Inputs may be any that keep to these rules, and one draw needn't show every extreme that they name: `pattern`: block column indices; one block row may name a column twice. `coarse_rows`: each row of a grid row's map names every coarse row once. `shared_lists`: each face's list names every row of the face once.
All inputs are finite; a program needn't handle non-finite values.
Results may differ from the reference program's by a relative error of at most 0.0085.
Values may be sent and summed in bfloat16 or wider, within the bound.
A program may use at most 64 MiB of HBM per device.

```python
import jax
import jax.numpy as jnp
from jax import lax

FACE = 512
BLK = 128
KNZ = 4
NPRIM = 64
NVEC = 128
NI = 2048
NB = 16
NCR = 512
N_SX = 4
N_SY = 8


def set_ends(values, key, smallest, largest):
    longest = values.shape.index(max(values.shape))
    spots = []
    for shift in (0, 1):
        where = [jax.random.randint(jax.random.fold_in(key, axis), (), 0, length) for axis, length in enumerate(values.shape)]
        where[longest] = (where[longest] + shift) % values.shape[longest]
        spots.append(tuple(where))
    return values.at[spots[0]].set(smallest).at[spots[1]].set(largest)


def levels(own_key, shape, cuts, smallest, top_value):
    loudness, own = 1.0, jax.random.fold_in(own_key, 6)
    for dim, parts in cuts:
        steps = jnp.exp(jax.random.uniform(jax.random.fold_in(own, dim), (parts,), jnp.float32, smallest / len(cuts), top_value / len(cuts)))
        loudness = loudness * jnp.repeat(steps, shape[dim] // parts).reshape([-1 if axis == dim else 1 for axis in range(len(shape))])
    return loudness


def centred(own_key, shape, deviation, most, cuts=(), kind=jnp.bfloat16):
    values = deviation * jax.random.normal(own_key, shape, jnp.float32)
    if cuts:
        values = values * levels(own_key, shape, cuts, -0.22, 0.18)
    return jnp.clip(values, -most, most).astype(kind)


def setup_inputs(seed: int = 0) -> dict:
    key_of = jax.random.split(jax.random.key(seed), 9)
    return {
        "residual": centred(key_of[0], (N_SX, N_SY, NI, NVEC), 1.0, 6.0, ((0, 4), (1, 8))),
        "weights": jnp.clip(1.0 + 0.18 * jax.random.normal(key_of[1], (N_SX, N_SY, NI), jnp.float32), 0.1, 1.9),
        "blocks": centred(key_of[2], (N_SX, N_SY, NB, KNZ, BLK, BLK), (BLK * KNZ) ** -0.5, 0.25, ((0, 4), (1, 8))),
        "pattern": set_ends(jax.random.randint(key_of[3], (N_SX, N_SY, NB, KNZ), 0, NB), jax.random.fold_in(key_of[3], 1), 0, NB - 1).astype(jnp.int32),
        "primal_basis": centred(key_of[4], (N_SX, N_SY, NI, NPRIM), (NI // 4) ** -0.5, 0.25, ((0, 4), (1, 8))),
        "coarse_inverse": centred(key_of[5], (N_SX, NCR, NCR), NCR ** -0.5, 0.25, ((0, 4), (1, 8)), jnp.float32),
        "coarse_rows": jax.vmap(lambda own: jax.random.permutation(own, NCR))(jax.random.split(key_of[6], N_SX)).reshape((N_SX, NCR)).astype(jnp.int32),
        "shared_lists": jax.vmap(lambda own: jax.random.permutation(own, FACE))(jax.random.split(key_of[7], N_SX * N_SY * 4)).reshape((N_SX, N_SY, 4, FACE)).astype(jnp.int32),
    }


def subdomain_part(items):
    residual, weights, blocks, pattern, primal_basis = items
    weighted = (weights[:, None] * residual.astype(jnp.float32)).astype(jnp.bfloat16)
    pieces = weighted.reshape(NB, BLK, NVEC)[pattern]
    solved = jnp.einsum('bkrc,bkcn->brn', blocks.astype(jnp.float32), pieces.astype(jnp.float32)).reshape(NI, NVEC)
    primal_vals = jnp.dot(primal_basis.T, weighted, preferred_element_type=jnp.float32)
    return solved, primal_vals


def place_rows(order, values):
    return jnp.zeros_like(values).at[order].set(values)


def pick_rows(values, order):
    return values[order]


def correct_part(items):
    solved, weights, primal_basis, primal_sol = items
    correction = jnp.dot(primal_basis, primal_sol, preferred_element_type=jnp.float32)
    return weights[:, None] * (solved + correction)


def reference(residual, weights, blocks, pattern, primal_basis, coarse_inverse, coarse_rows, shared_lists):
    count = N_SX * N_SY
    flat_w = weights.reshape(count, NI)
    flat_basis = primal_basis.reshape(count, NI, NPRIM)
    solved, primal_vals = lax.map(subdomain_part, (residual.reshape(count, NI, NVEC), flat_w, blocks.reshape(count, NB, KNZ, BLK, BLK), pattern.reshape(count, NB, KNZ), flat_basis))
    primal_vals = primal_vals.reshape(N_SX, NCR, NVEC)
    coarse_rhs = jax.vmap(place_rows)(coarse_rows, primal_vals)
    coarse_sol = jnp.einsum('imn,inv->imv', coarse_inverse, coarse_rhs, precision=lax.Precision.HIGHEST)
    primal_sol = jax.vmap(pick_rows)(coarse_sol, coarse_rows).astype(jnp.bfloat16).reshape(count, NPRIM, NVEC)
    value = lax.map(correct_part, (solved, flat_w, flat_basis, primal_sol))
    value = value.reshape(N_SX, N_SY, 4, FACE, NVEC)
    from_north = jnp.pad(value[:-1, :, 1], ((1, 0), (0, 0), (0, 0), (0, 0)))
    from_south = jnp.pad(value[1:, :, 0], ((0, 1), (0, 0), (0, 0), (0, 0)))
    from_west = jnp.pad(value[:, :-1, 3], ((0, 0), (1, 0), (0, 0), (0, 0)))
    from_east = jnp.pad(value[:, 1:, 2], ((0, 0), (0, 1), (0, 0), (0, 0)))
    picker = jax.vmap(jax.vmap(pick_rows))
    across = jnp.stack([picker(from_north, shared_lists[:, :, 0]), picker(from_south, shared_lists[:, :, 1]), picker(from_west, shared_lists[:, :, 2]), picker(from_east, shared_lists[:, :, 3])], axis=2)
    total = value + across
    return total.reshape(N_SX, N_SY, NI, NVEC).astype(jnp.bfloat16)
```

```python
import functools

import jax
import jax.numpy as jnp
from jax import lax
from jax.experimental import pallas as pl
from jax.experimental.pallas import tpu as pltpu
from jax.sharding import PartitionSpec as P

MESH = pl.DeviceIdType.MESH
F32 = jnp.float32
BF16 = jnp.bfloat16
LANES = 128
OPPOSITE = (1, 0, 3, 2)


def down_rows(row):
    return jnp.broadcast_to(row, (LANES, LANES)).T


def kernel(
    n_sx, n_sy,
    res_hbm, w_ref, blocks_hbm, pat_ref, basis_hbm, inv_hbm, ord_ref, sh_ref,
    out_hbm,
    res, basis, blocks, inv, wcol, weighted, acc, comb, onehot, inv_perm, pick, cols,
    gath, csol, psol, face_out, basis_out, face_in, basis_in, psol_in, out,
    in_sem, blk_sem, out_sem, pv_s, pv_r, cs_s, cs_r, fb_s, fb_r, fw_s, fw_r, ps_s, ps_r,
):
    i, j = lax.axis_index("sx"), lax.axis_index("sy")
    nb, knz, blk, _ = blocks.shape
    nprim, ncr = inv.shape
    ni, nvec = res.shape
    face = ni // 4
    per = face // blk

    load_basis = pltpu.make_async_copy(basis_hbm, basis, in_sem.at[0])
    load_res = pltpu.make_async_copy(res_hbm, res, in_sem.at[1])
    load_inv = pltpu.make_async_copy(inv_hbm, inv, in_sem.at[2])
    load_blocks = [
        pltpu.make_async_copy(
            blocks_hbm.at[pl.ds(f * per, per)], blocks.at[pl.ds(f * per, per)], blk_sem.at[f]
        )
        for f in range(4)
    ]
    load_basis.start()
    load_res.start()
    load_inv.start()
    for copy in load_blocks:
        copy.start()

    has = (i > 0, i < n_sx - 1, j > 0, j < n_sy - 1)
    there = ((i - 1, j), (i + 1, j), (i, j - 1), (i, j + 1))

    barrier = pltpu.get_barrier_semaphore()

    def greet(step, carry):
        peer = lax.rem(j + step, n_sy)
        pl.semaphore_signal(barrier, inc=1, device_id=(i, peer), device_id_type=MESH)
        return carry

    lax.fori_loop(1, n_sy, greet, 0)
    for f in (0, 1):

        @pl.when(has[f])
        def _():
            pl.semaphore_signal(barrier, inc=1, device_id=there[f], device_id_type=MESH)

    def basis_copy(f):
        return pltpu.make_async_remote_copy(
            src_ref=basis_out.at[f], dst_ref=basis_in.at[OPPOSITE[f]],
            send_sem=fb_s.at[f], recv_sem=fb_r.at[OPPOSITE[f]],
            device_id=there[f], device_id_type=MESH,
        )

    def face_copy(f):
        return pltpu.make_async_remote_copy(
            src_ref=face_out.at[f], dst_ref=face_in.at[OPPOSITE[f]],
            send_sem=fw_s.at[f], recv_sem=fw_r.at[OPPOSITE[f]],
            device_id=there[f], device_id_type=MESH,
        )

    def psol_copy(f):
        return pltpu.make_async_remote_copy(
            src_ref=psol.at[0], dst_ref=psol_in.at[OPPOSITE[f]],
            send_sem=ps_s.at[f], recv_sem=ps_r.at[OPPOSITE[f]],
            device_id=there[f], device_id_type=MESH,
        )

    def rows_copy(buf, send, recv, peer, slot):
        rows = pl.ds(pl.multiple_of(slot * nprim, nprim), nprim)
        return pltpu.make_async_remote_copy(
            src_ref=buf.at[rows], dst_ref=buf.at[rows],
            send_sem=send.at[peer], recv_sem=recv.at[slot],
            device_id=(i, peer), device_id_type=MESH,
        )

    def send_rows(buf, send, recv):
        def step(d, carry):
            rows_copy(buf, send, recv, lax.rem(j + d, n_sy), j).start()
            return carry

        lax.fori_loop(1, n_sy, step, 0)

    def wait_rows(buf, send, recv):
        def step(d, carry):
            peer = lax.rem(j + d, n_sy)
            rows_copy(buf, send, recv, peer, peer).wait_recv()
            return carry

        lax.fori_loop(1, n_sy, step, 0)

    def drain_rows(buf, send, recv):
        def step(d, carry):
            rows_copy(buf, send, recv, lax.rem(j + d, n_sy), j).wait_send()
            return carry

        lax.fori_loop(1, n_sy, step, 0)

    for f in range(4):

        @pl.when(jnp.logical_not(has[f]))
        def _():
            face_in[f] = jnp.zeros(face_in.shape[1:], BF16)
            basis_in[f] = jnp.zeros(basis_in.shape[1:], BF16)
            if f < 2:
                psol_in[f] = jnp.zeros(psol_in.shape[1:], BF16)

    for b in range(nb):
        wcol[b] = down_rows(w_ref[0:1, b * blk : (b + 1) * blk])
    load_basis.wait()
    load_res.wait()
    for b in range(nb):
        rows = slice(b * blk, (b + 1) * blk)
        weighted[b] = (wcol[b] * res[rows, :].astype(F32)).astype(BF16)
    pv = lax.dot_general(
        basis[...], weighted[...].reshape(ni, nvec), (((0,), (0,)), ((), ())),
        preferred_element_type=F32,
    )
    own = pl.ds(pl.multiple_of(j * nprim, nprim), nprim)
    gath[own, :] = pv.astype(BF16)

    pl.semaphore_wait(
        barrier, n_sy - 1 + has[0].astype(jnp.int32) + has[1].astype(jnp.int32)
    )
    send_rows(gath, pv_s, pv_r)

    half = per // 2
    for f in range(4):
        parts = []
        for b in range(f * per, (f + 1) * per):
            rows = slice(b * blk, (b + 1) * blk)
            parts.append(wcol[b][:, :nprim] * basis[rows, :].astype(F32))
        zero = jnp.zeros((blk, LANES - nprim), F32)
        for p in range(per):
            comb[f, p * blk : (p + 1) * blk, :] = jnp.concatenate([parts[p], zero], axis=1)
        for p in range(half):
            both = jnp.concatenate([parts[p], parts[p + half]], axis=1)
            basis_out[f, p * blk : (p + 1) * blk, :] = both.astype(BF16)

        @pl.when(has[f])
        def _():
            basis_copy(f).start()

    for f in range(4):
        load_blocks[f].wait()
        for b in range(f * per, (f + 1) * per):
            left = jnp.concatenate([blocks[b, k] for k in range(knz)], axis=1)
            right = jnp.concatenate([weighted[pat_ref[b, k]] for k in range(knz)], axis=0)
            solved = wcol[b] * jnp.dot(left, right, preferred_element_type=F32)
            rows = slice(b * blk, (b + 1) * blk)
            acc[rows, :] = solved
            face_out[f, (b - f * per) * blk : (b - f * per + 1) * blk, :] = solved.astype(BF16)

        @pl.when(has[f])
        def _():
            face_copy(f).start()

    load_inv.wait()
    chunk = 512 if ncr <= 512 else LANES
    inv16 = inv[...].astype(BF16)

    def permute_columns(c, carry):
        at = pl.ds(pl.multiple_of(c * chunk, chunk), chunk)
        hit = lax.broadcasted_iota(jnp.int32, (ncr, chunk), 0) == ord_ref[:, at]
        inv_perm[:, at] = jnp.dot(
            inv16, jnp.where(hit, 1.0, 0.0).astype(BF16), preferred_element_type=F32
        ).astype(BF16)
        return carry

    lax.fori_loop(0, ncr // chunk, permute_columns, 0)

    wait_rows(gath, pv_s, pv_r)
    csol[own, :] = jnp.dot(
        inv_perm[...], gath[...], preferred_element_type=F32
    ).astype(BF16)
    send_rows(csol, cs_s, cs_r)

    wide = LANES // nprim
    lane = lax.broadcasted_iota(jnp.int32, (nprim, LANES), 1).astype(F32)
    for m, who in enumerate((j, jnp.maximum(j - 1, 0), jnp.minimum(j + 1, n_sy - 1))):
        at = pl.ds(pl.multiple_of((who // wide) * LANES, LANES), LANES)
        cols[m] = down_rows(ord_ref[:, at].astype(F32))
        col = cols[m, pl.ds(pl.multiple_of((who % wide) * nprim, nprim), nprim), :]
        for c in range(ncr // LANES):
            pick[m * nprim : (m + 1) * nprim, c * LANES : (c + 1) * LANES] = jnp.where(
                col == lane + float(c * LANES), 1.0, 0.0
            ).astype(BF16)

    wide_lane = lax.broadcasted_iota(jnp.int32, (LANES, face), 1).astype(F32)
    for f in range(4):
        for c in range(face // LANES):
            at = slice(c * LANES, (c + 1) * LANES)
            col = down_rows(sh_ref[f : f + 1, at].astype(F32))
            col = jnp.concatenate([col] * (face // LANES), axis=1)
            onehot[f, at, :] = jnp.where(col == wide_lane, 1.0, 0.0).astype(BF16)

    upper = lax.broadcasted_iota(jnp.int32, (face // 2, LANES), 1) >= nprim
    for f in range(4):

        @pl.when(has[f])
        def _():
            g = OPPOSITE[f]
            basis_copy(g).wait_recv()
            face_copy(g).wait_recv()

        packed = basis_in[f].astype(F32)
        first = jnp.concatenate(
            [jnp.zeros((face // 2, LANES - nprim), F32), packed[:, :nprim]], axis=1
        )
        second = jnp.where(upper, packed, 0.0)
        theirs = jnp.concatenate([first, second], axis=0).astype(BF16)
        moved = jnp.dot(
            onehot[f], jnp.concatenate([face_in[f], theirs], axis=1),
            preferred_element_type=F32,
        )
        rows = slice(f * face, (f + 1) * face)
        acc[rows, :] = acc[rows, :] + moved[:, :nvec]
        comb[f] = comb[f] + moved[:, nvec:]

    wait_rows(csol, cs_s, cs_r)
    taken = jnp.dot(pick[...], csol[...], preferred_element_type=F32).astype(BF16)
    for m in range(3):
        psol[m] = taken[m * nprim : (m + 1) * nprim, :]
    for f in (0, 1):

        @pl.when(has[f])
        def _():
            psol_copy(f).start()

    for f in (2, 3, 0, 1):
        if f < 2:

            @pl.when(has[f])
            def _():
                psol_copy(OPPOSITE[f]).wait_recv()

        other = psol_in[f] if f < 2 else psol[f - 1]
        both = jnp.concatenate([psol[0], other], axis=0)
        rows = slice(f * face, (f + 1) * face)
        out[rows, :] = (
            acc[rows, :]
            + jnp.dot(comb[f].astype(BF16), both, preferred_element_type=F32)
        ).astype(BF16)
        pltpu.make_async_copy(out.at[rows], out_hbm.at[rows], out_sem.at[f]).start()

    drain_rows(gath, pv_s, pv_r)
    drain_rows(csol, cs_s, cs_r)
    for f in range(4):

        @pl.when(has[f])
        def _():
            basis_copy(f).wait_send()
            face_copy(f).wait_send()
            if f < 2:
                psol_copy(f).wait_send()

        rows = slice(f * face, (f + 1) * face)
        pltpu.make_async_copy(out.at[rows], out_hbm.at[rows], out_sem.at[f]).wait()


def body(
    n_sx, n_sy,
    residual, weights, blocks, pattern, primal_basis, coarse_inverse, coarse_rows, shared_lists,
):
    ni, nvec = residual.shape[2:]
    nb, knz, blk = blocks.shape[2:5]
    nprim = primal_basis.shape[-1]
    ncr = coarse_rows.shape[-1]
    face = shared_lists.shape[-1]
    vmem, smem, hbm = (
        pl.BlockSpec(memory_space=space) for space in (pltpu.VMEM, pltpu.SMEM, pl.ANY)
    )
    dma = pltpu.SemaphoreType.DMA
    total = pl.pallas_call(
        functools.partial(kernel, n_sx, n_sy),
        out_shape=jax.ShapeDtypeStruct((ni, nvec), BF16),
        in_specs=[hbm, vmem, hbm, smem, hbm, hbm, vmem, vmem],
        out_specs=hbm,
        scratch_shapes=[
            pltpu.VMEM((ni, nvec), BF16),
            pltpu.VMEM((ni, nprim), BF16),
            pltpu.VMEM((nb, knz, blk, blk), BF16),
            pltpu.VMEM((nprim, ncr), F32),
            pltpu.VMEM((nb, blk, LANES), F32),
            pltpu.VMEM((nb, blk, nvec), BF16),
            pltpu.VMEM((ni, nvec), F32),
            pltpu.VMEM((4, face, LANES), F32),
            pltpu.VMEM((4, face, face), BF16),
            pltpu.VMEM((nprim, ncr), BF16),
            pltpu.VMEM((3 * nprim, ncr), BF16),
            pltpu.VMEM((3, LANES, LANES), F32),
            pltpu.VMEM((ncr, nvec), BF16),
            pltpu.VMEM((ncr, nvec), BF16),
            pltpu.VMEM((3, nprim, nvec), BF16),
            pltpu.VMEM((4, face, nvec), BF16),
            pltpu.VMEM((4, face // 2, LANES), BF16),
            pltpu.VMEM((4, face, nvec), BF16),
            pltpu.VMEM((4, face // 2, LANES), BF16),
            pltpu.VMEM((2, nprim, nvec), BF16),
            pltpu.VMEM((ni, nvec), BF16),
            dma((3,)), dma((4,)), dma((4,)),
            dma((n_sy,)), dma((n_sy,)), dma((n_sy,)), dma((n_sy,)),
            dma((4,)), dma((4,)), dma((4,)), dma((4,)), dma((2,)), dma((2,)),
        ],
        compiler_params=pltpu.CompilerParams(
            collective_id=0, has_side_effects=True, vmem_limit_bytes=40 * 1024 * 1024
        ),
    )(
        residual[0, 0], weights[0], blocks[0, 0], pattern[0, 0], primal_basis[0, 0],
        coarse_inverse[0], coarse_rows, shared_lists[0, 0],
    )
    return total[None, None]


def solution(mesh):
    return jax.shard_map(
        functools.partial(body, mesh.shape["sx"], mesh.shape["sy"]),
        mesh=mesh,
        in_specs=(
            P("sx", "sy", None, None),
            P("sx", "sy", None),
            P("sx", "sy", None, None, None, None),
            P("sx", "sy", None, None),
            P("sx", "sy", None, None),
            P("sx", "sy", None),
            P("sx", None),
            P("sx", "sy", None, None),
        ),
        out_specs=P("sx", "sy", None, None),
        check_vma=False,
    )
```

```python
import functools

import jax
import jax.numpy as jnp
from jax import lax
from jax.experimental import pallas as pl
from jax.experimental.pallas import tpu as pltpu
from jax.sharding import PartitionSpec as P

MESH = pl.DeviceIdType.MESH
F32 = jnp.float32
BF16 = jnp.bfloat16
LANES = 128
OPPOSITE = (1, 0, 3, 2)


def down_rows(row):
    return jnp.broadcast_to(row, (LANES, LANES)).T


def kernel(
    n_sx, n_sy,
    res_hbm, w_hbm, blocks_hbm, pat_hbm, basis_hbm, inv_hbm, ord_hbm, sh_hbm,
    out_hbm,
    res, w_ref, basis, blocks, inv, ord_ref, sh_ref, pat_ref,
    wcol, weighted, acc, comb, onehot, inv_perm, pick, cols,
    gath, csol, psol, face_out, basis_out, face_in, basis_in, psol_in, out,
    in_sem, blk_sem, out_sem, pv_s, pv_r, cs_s, cs_r, fb_s, fb_r, fw_s, fw_r, ps_s, ps_r,
):
    i, j = lax.axis_index("sx"), lax.axis_index("sy")
    nb, knz, blk, _ = blocks.shape
    nprim, ncr = inv.shape
    ni, nvec = res.shape
    face = ni // 4
    per = face // blk

    loads = [
        pltpu.make_async_copy(source, target, in_sem.at[n])
        for n, (source, target) in enumerate(
            (
                (w_hbm, w_ref), (basis_hbm, basis), (res_hbm, res), (ord_hbm, ord_ref),
                (sh_hbm, sh_ref), (pat_hbm, pat_ref), (inv_hbm, inv),
            )
        )
    ]
    load_w, load_basis, load_res, load_ord, load_sh, load_pat, load_inv = loads
    load_blocks = [
        pltpu.make_async_copy(
            blocks_hbm.at[pl.ds(f * per, per)], blocks.at[pl.ds(f * per, per)], blk_sem.at[f]
        )
        for f in range(4)
    ]
    for copy in loads + load_blocks:
        copy.start()

    has = (i > 0, i < n_sx - 1, j > 0, j < n_sy - 1)
    there = ((i - 1, j), (i + 1, j), (i, j - 1), (i, j + 1))

    barrier = pltpu.get_barrier_semaphore()

    def greet(step, carry):
        peer = lax.rem(j + step, n_sy)
        pl.semaphore_signal(barrier, inc=1, device_id=(i, peer), device_id_type=MESH)
        return carry

    lax.fori_loop(1, n_sy, greet, 0)
    for f in (0, 1):

        @pl.when(has[f])
        def _():
            pl.semaphore_signal(barrier, inc=1, device_id=there[f], device_id_type=MESH)

    def basis_copy(f):
        return pltpu.make_async_remote_copy(
            src_ref=basis_out.at[f], dst_ref=basis_in.at[OPPOSITE[f]],
            send_sem=fb_s.at[f], recv_sem=fb_r.at[OPPOSITE[f]],
            device_id=there[f], device_id_type=MESH,
        )

    def face_copy(f):
        return pltpu.make_async_remote_copy(
            src_ref=face_out.at[f], dst_ref=face_in.at[OPPOSITE[f]],
            send_sem=fw_s.at[f], recv_sem=fw_r.at[OPPOSITE[f]],
            device_id=there[f], device_id_type=MESH,
        )

    def psol_copy(f):
        return pltpu.make_async_remote_copy(
            src_ref=psol.at[0], dst_ref=psol_in.at[OPPOSITE[f]],
            send_sem=ps_s.at[f], recv_sem=ps_r.at[OPPOSITE[f]],
            device_id=there[f], device_id_type=MESH,
        )

    def rows_copy(buf, send, recv, peer, slot):
        rows = pl.ds(pl.multiple_of(slot * nprim, nprim), nprim)
        return pltpu.make_async_remote_copy(
            src_ref=buf.at[rows], dst_ref=buf.at[rows],
            send_sem=send.at[peer], recv_sem=recv.at[slot],
            device_id=(i, peer), device_id_type=MESH,
        )

    def send_rows(buf, send, recv):
        def step(d, carry):
            rows_copy(buf, send, recv, lax.rem(j + d, n_sy), j).start()
            return carry

        lax.fori_loop(1, n_sy, step, 0)

    def wait_rows(buf, send, recv):
        def step(d, carry):
            peer = lax.rem(j + d, n_sy)
            rows_copy(buf, send, recv, peer, peer).wait_recv()
            return carry

        lax.fori_loop(1, n_sy, step, 0)

    def drain_rows(buf, send, recv):
        def step(d, carry):
            rows_copy(buf, send, recv, lax.rem(j + d, n_sy), j).wait_send()
            return carry

        lax.fori_loop(1, n_sy, step, 0)

    for f in range(4):

        @pl.when(jnp.logical_not(has[f]))
        def _():
            face_in[f] = jnp.zeros(face_in.shape[1:], BF16)
            basis_in[f] = jnp.zeros(basis_in.shape[1:], BF16)
            if f < 2:
                psol_in[f] = jnp.zeros(psol_in.shape[1:], BF16)

    load_w.wait()
    load_basis.wait()
    for f in range(4):
        at = slice(f * face, (f + 1) * face)
        basis_out[f] = (w_ref[0:1, at] * basis[:, at].astype(F32)).astype(BF16)
    load_res.wait()
    pv = jnp.zeros((nprim, nvec), F32)
    for f in range(4):
        pv += jnp.dot(
            basis_out[f], res[f * face : (f + 1) * face, :], preferred_element_type=F32
        )
    own = pl.ds(pl.multiple_of(j * nprim, nprim), nprim)
    gath[own, :] = pv.astype(BF16)

    pl.semaphore_wait(
        barrier, n_sy - 1 + has[0].astype(jnp.int32) + has[1].astype(jnp.int32)
    )
    send_rows(gath, pv_s, pv_r)
    for f in range(4):

        @pl.when(has[f])
        def _():
            basis_copy(f).start()

    for b in range(nb):
        rows = slice(b * blk, (b + 1) * blk)
        wcol[b] = down_rows(w_ref[0:1, rows])
        weighted[b] = (wcol[b] * res[rows, :].astype(F32)).astype(BF16)

    load_pat.wait()
    for f in range(4):
        load_blocks[f].wait()
        for b in range(f * per, (f + 1) * per):
            left = jnp.concatenate([blocks[b, k] for k in range(knz)], axis=1)
            right = jnp.concatenate([weighted[pat_ref[k, b]] for k in range(knz)], axis=0)
            solved = wcol[b] * jnp.dot(left, right, preferred_element_type=F32)
            rows = slice(b * blk, (b + 1) * blk)
            acc[rows, :] = solved
            face_out[f, (b - f * per) * blk : (b - f * per + 1) * blk, :] = solved.astype(BF16)

        @pl.when(has[f])
        def _():
            face_copy(f).start()

    load_inv.wait()
    load_ord.wait()
    load_sh.wait()
    chunk = 512 if ncr <= 512 else LANES
    inv16 = inv[...].astype(BF16)

    def permute_columns(c, carry):
        at = pl.ds(pl.multiple_of(c * chunk, chunk), chunk)
        hit = lax.broadcasted_iota(jnp.int32, (ncr, chunk), 0) == ord_ref[:, at]
        inv_perm[:, at] = jnp.dot(
            inv16, jnp.where(hit, 1.0, 0.0).astype(BF16), preferred_element_type=F32
        ).astype(BF16)
        return carry

    lax.fori_loop(0, ncr // chunk, permute_columns, 0)

    wait_rows(gath, pv_s, pv_r)
    csol[own, :] = jnp.dot(
        inv_perm[...], gath[...], preferred_element_type=F32
    ).astype(BF16)
    send_rows(csol, cs_s, cs_r)

    wide = LANES // nprim
    lane = lax.broadcasted_iota(jnp.int32, (nprim, LANES), 1).astype(F32)
    for m, who in enumerate((j, jnp.maximum(j - 1, 0), jnp.minimum(j + 1, n_sy - 1))):
        at = pl.ds(pl.multiple_of((who // wide) * LANES, LANES), LANES)
        cols[m] = down_rows(ord_ref[:, at].astype(F32))
        col = cols[m, pl.ds(pl.multiple_of((who % wide) * nprim, nprim), nprim), :]
        for c in range(ncr // LANES):
            pick[m * nprim : (m + 1) * nprim, c * LANES : (c + 1) * LANES] = jnp.where(
                col == lane + float(c * LANES), 1.0, 0.0
            ).astype(BF16)

    wide_lane = lax.broadcasted_iota(jnp.int32, (LANES, face), 1).astype(F32)
    for f in range(4):
        for c in range(face // LANES):
            at = slice(c * LANES, (c + 1) * LANES)
            col = down_rows(sh_ref[f : f + 1, at].astype(F32))
            col = jnp.concatenate([col] * (face // LANES), axis=1)
            onehot[f, at, :] = jnp.where(col == wide_lane, 1.0, 0.0).astype(BF16)

    for f in range(4):

        @pl.when(has[f])
        def _():
            g = OPPOSITE[f]
            basis_copy(g).wait_recv()
            face_copy(g).wait_recv()

        rows = slice(f * face, (f + 1) * face)
        acc[rows, :] = acc[rows, :] + jnp.dot(
            onehot[f], face_in[f], preferred_element_type=F32
        )
        moved = lax.dot_general(
            basis_in[f], onehot[f], (((1,), (1,)), ((), ())), preferred_element_type=F32
        )
        both = jnp.concatenate([basis_out[f].astype(F32), moved], axis=0)
        comb[f] = both.T.astype(BF16)

    wait_rows(csol, cs_s, cs_r)
    taken = jnp.dot(pick[...], csol[...], preferred_element_type=F32).astype(BF16)
    for m in range(3):
        psol[m] = taken[m * nprim : (m + 1) * nprim, :]
    for f in (0, 1):

        @pl.when(has[f])
        def _():
            psol_copy(f).start()

    for f in (2, 3, 0, 1):
        if f < 2:

            @pl.when(has[f])
            def _():
                psol_copy(OPPOSITE[f]).wait_recv()

        other = psol_in[f] if f < 2 else psol[f - 1]
        both = jnp.concatenate([psol[0], other], axis=0)
        rows = slice(f * face, (f + 1) * face)
        out[rows, :] = (
            acc[rows, :]
            + jnp.dot(comb[f], both, preferred_element_type=F32)
        ).astype(BF16)
        pltpu.make_async_copy(out.at[rows], out_hbm.at[rows], out_sem.at[f]).start()

    drain_rows(gath, pv_s, pv_r)
    drain_rows(csol, cs_s, cs_r)
    for f in range(4):

        @pl.when(has[f])
        def _():
            basis_copy(f).wait_send()
            face_copy(f).wait_send()
            if f < 2:
                psol_copy(f).wait_send()

        rows = slice(f * face, (f + 1) * face)
        pltpu.make_async_copy(out.at[rows], out_hbm.at[rows], out_sem.at[f]).wait()


def body(
    n_sx, n_sy,
    residual, weights, blocks, pattern, primal_basis, coarse_inverse, coarse_rows, shared_lists,
):
    ni, nvec = residual.shape[2:]
    nb, knz, blk = blocks.shape[2:5]
    nprim = primal_basis.shape[-1]
    ncr = coarse_rows.shape[-1]
    face = shared_lists.shape[-1]
    hbm = pl.BlockSpec(memory_space=pltpu.HBM)
    dma = pltpu.SemaphoreType.DMA
    total = pl.pallas_call(
        functools.partial(kernel, n_sx, n_sy),
        out_shape=jax.ShapeDtypeStruct((ni, nvec), BF16),
        in_specs=[hbm] * 8,
        out_specs=hbm,
        scratch_shapes=[
            pltpu.VMEM((ni, nvec), BF16),
            pltpu.VMEM((1, ni), F32),
            pltpu.VMEM((nprim, ni), BF16),
            pltpu.VMEM((nb, knz, blk, blk), BF16),
            pltpu.VMEM((nprim, ncr), F32),
            pltpu.VMEM((1, ncr), jnp.int32),
            pltpu.VMEM((4, face), jnp.int32),
            pltpu.SMEM((knz, nb), jnp.int32),
            pltpu.VMEM((nb, blk, LANES), F32),
            pltpu.VMEM((nb, blk, nvec), BF16),
            pltpu.VMEM((ni, nvec), F32),
            pltpu.VMEM((4, face, 2 * nprim), BF16),
            pltpu.VMEM((4, face, face), BF16),
            pltpu.VMEM((nprim, ncr), BF16),
            pltpu.VMEM((3 * nprim, ncr), BF16),
            pltpu.VMEM((3, LANES, LANES), F32),
            pltpu.VMEM((ncr, nvec), BF16),
            pltpu.VMEM((ncr, nvec), BF16),
            pltpu.VMEM((3, nprim, nvec), BF16),
            pltpu.VMEM((4, face, nvec), BF16),
            pltpu.VMEM((4, nprim, face), BF16),
            pltpu.VMEM((4, face, nvec), BF16),
            pltpu.VMEM((4, nprim, face), BF16),
            pltpu.VMEM((2, nprim, nvec), BF16),
            pltpu.VMEM((ni, nvec), BF16),
            dma((7,)), dma((4,)), dma((4,)),
            dma((n_sy,)), dma((n_sy,)), dma((n_sy,)), dma((n_sy,)),
            dma((4,)), dma((4,)), dma((4,)), dma((4,)), dma((2,)), dma((2,)),
        ],
        compiler_params=pltpu.CompilerParams(
            collective_id=0, has_side_effects=True, vmem_limit_bytes=64 * 1024 * 1024
        ),
    )(
        residual[0, 0], weights[0], blocks[0, 0], pattern[0, 0].T, primal_basis[0, 0].T,
        coarse_inverse[0], coarse_rows, shared_lists[0, 0],
    )
    return total[None, None]


def solution(mesh):
    return jax.shard_map(
        functools.partial(body, mesh.shape["sx"], mesh.shape["sy"]),
        mesh=mesh,
        in_specs=(
            P("sx", "sy", None, None),
            P("sx", "sy", None),
            P("sx", "sy", None, None, None, None),
            P("sx", "sy", None, None),
            P("sx", "sy", None, None),
            P("sx", "sy", None),
            P("sx", None),
            P("sx", "sy", None, None),
        ),
        out_specs=P("sx", "sy", None, None),
        check_vma=False,
    )
```
